32 devices in a mesh: groups: 2 (over y), refs: 8 (over z, x), parts: 2 (over core).
Axes of the slice: x: 2, y: 2, z: 4, core: 2. Of those that a mesh axis runs over, the one named last changes fastest.
Arguments:
- particles: float32 [128, 16384], P(('groups', 'parts')), parts along dimension 0, may hold values from -24 to 24
- references: float32 [64, 16384], P(('groups', 'refs')), parts along dimension 0, may hold values from -6 to 6
- shift_offsets: int32 [50, 2], P('groups'), parts along dimension 0, may hold values from -4 to 4, as said below
- particle_group: int32 [128], P(('groups', 'parts')), parts along dimension 0, may hold values from 0 to 15
- group_scale: float32 [16], replicated, may hold values from 0.7 to 1.4
Outputs:
- posterior_mean: float32 [128, 16384], P(('groups', 'parts'), 'refs'), parts along dimension 0
- ref_sums: float32 [64, 16384], P(('groups', 'refs'), 'parts'), parts along dimension 0
The draws below stay inside these ranges and needn't reach their ends.
There are 2 independent parts, one for each index of `groups`. The reference program is written for one: setup_inputs(seed, part) draws one part's arguments, and reference() takes and returns one part's arrays. A program takes and returns all parts, laid end to end along the dimension named above; an argument that names none is the same for every part. Nothing has to cross between parts.
Inputs may be any that keep to these rules, and one draw needn't show every extreme that they name: `shift_offsets`: 25 distinct (row, column) pairs.
All inputs are finite; a program needn't handle non-finite values.
Results may differ from the reference program's by a relative error of at most 0.0003.
Values sent between devices are 32-bit elements; how exact they have to be, the bound alone decides.
No kernel may reach another device: no remote copies, remote signals or barrier semaphores. Data moves between devices by JAX's collectives and lax.ppermute only.
A program may use at most 64 MiB of HBM per device.

```python
import math
import jax
import jax.numpy as jnp
from jax import lax

BOX = 128
PIX = 16384
SHIFTS = 25
OFFSET_RANGE = 4
NGROUPS = 16
K = 32
P_SIZE = 64


def draw_references(key, part):
    values = jax.random.normal(jax.random.fold_in(key, 12), (K, PIX), jnp.float32)
    return jnp.clip(values, -6.0, 6.0)


def draw_shift_offsets(key, part):
    span_size = 2 * OFFSET_RANGE + 1
    picks = jax.random.permutation(jax.random.fold_in(key, 11), span_size * span_size)[:SHIFTS]
    return jnp.stack([picks // span_size - OFFSET_RANGE, picks % span_size - OFFSET_RANGE], axis=1).astype(jnp.int32)


def shift_single(image_flat, offset_pair):
    grid = image_flat.reshape(BOX, BOX)
    return jnp.roll(grid, (offset_pair[0], offset_pair[1]), axis=(0, 1)).reshape(PIX)


def draw_particles(key, part):
    plant_count = 16
    bank_images = draw_references(key, part)
    offset_table = draw_shift_offsets(key, part)
    subkeys = jax.random.split(jax.random.fold_in(key, 13), 7)
    first_ref = jax.random.randint(subkeys[0], (P_SIZE, plant_count), 0, K)
    step_ref = jax.random.randint(subkeys[6], (P_SIZE,), 1, K)
    which_ref = first_ref.at[:, 1].set((first_ref[:, 0] + step_ref) % K)
    which_shift = jax.random.randint(subkeys[1], (P_SIZE, plant_count), 0, SHIFTS)
    targets = jax.random.uniform(subkeys[2], (P_SIZE, plant_count), jnp.float32, 6.0, 12.0)
    noise_field = jax.random.normal(subkeys[5], (P_SIZE, PIX), jnp.float32)

    def add_plant(plant_index, running):
        picked = bank_images[which_ref[:, plant_index]]
        pair_rows = offset_table[which_shift[:, plant_index]]
        moved_images = jax.vmap(shift_single)(picked, pair_rows)
        length = jnp.sqrt(jnp.sum(moved_images * moved_images, axis=1, keepdims=True))
        return running + moved_images * targets[:, plant_index][:, None] / length
    particle_field = lax.fori_loop(0, plant_count, add_plant, noise_field)
    return jnp.clip(particle_field, -24.0, 24.0)


def place_ends(values, own_key, low, high):
    index_at = [jax.random.randint(jax.random.fold_in(own_key, axis), (), 0, length) for axis, length in enumerate(values.shape)]
    main_axis = values.shape.index(max(values.shape))
    next_to = index_at[:main_axis] + [(index_at[main_axis] + 1) % values.shape[main_axis]] + index_at[main_axis + 1:]
    return values.at[tuple(index_at)].set(low).at[tuple(next_to)].set(high)


def setup_inputs(seed: int = 0, part: int = 0) -> dict:
    keys = jax.random.split(jax.random.key(seed), 6)
    own_keys = jax.random.split(jax.random.fold_in(keys[5], part), 6)
    particles = draw_particles(jax.random.fold_in(jax.random.fold_in(keys[5], part), 71), part)
    references = draw_references(jax.random.fold_in(jax.random.fold_in(keys[5], part), 71), part)
    shift_offsets = draw_shift_offsets(jax.random.fold_in(jax.random.fold_in(keys[5], part), 71), part)
    particle_group = place_ends(jax.random.randint(own_keys[3], (P_SIZE,), 0, NGROUPS), jax.random.fold_in(own_keys[3], 1), 0, NGROUPS - 1).astype(jnp.int32)
    group_scale = jnp.clip(jnp.exp(jax.random.uniform(keys[4], (NGROUPS,), jnp.float32, math.log(0.7), math.log(1.4))), 0.7, 1.4)
    return dict(particles=particles, references=references, shift_offsets=shift_offsets, particle_group=particle_group, group_scale=group_scale)


def move_images(images, offset_pair, sign):
    grid = images.reshape(-1, BOX, BOX)
    moved_grid = jnp.roll(grid, (sign * offset_pair[0], sign * offset_pair[1]), axis=(1, 2))
    return moved_grid.reshape(-1, PIX)


def reference(particles, references, shift_offsets, particle_group, group_scale):
    membership = (particle_group[:, None] == jnp.arange(NGROUPS, dtype=jnp.int32)[None, :]).astype(jnp.float32)
    score_scale = jnp.dot(membership, group_scale, precision=lax.Precision.HIGHEST, preferred_element_type=jnp.float32) / BOX

    def shift_scores(offset_pair):
        shifted = move_images(particles, offset_pair, -1)
        return lax.dot_general(shifted, references, (((1,), (1,)), ((), ())), precision=lax.Precision.HIGHEST, preferred_element_type=jnp.float32)

    scores = lax.map(shift_scores, shift_offsets) * score_scale[None, :, None]
    peak_value = jnp.max(scores, axis=(0, 2))
    expo = jnp.exp(scores - peak_value[None, :, None])
    total_mass = jnp.sum(expo, axis=(0, 2))
    weights = expo / total_mass[None, :, None]

    def accumulate(running, inputs):
        offset_pair, chosen = inputs
        mean_sum, ref_sum = running
        image_part = jnp.dot(chosen, references, precision=lax.Precision.HIGHEST, preferred_element_type=jnp.float32)
        mean_sum = mean_sum + move_images(image_part, offset_pair, 1)
        aligned = move_images(particles, offset_pair, -1)
        ref_sum = ref_sum + lax.dot_general(chosen, aligned, (((0,), (0,)), ((), ())), precision=lax.Precision.HIGHEST, preferred_element_type=jnp.float32)
        return (mean_sum, ref_sum), None

    start = (jnp.zeros(particles.shape, jnp.float32), jnp.zeros(references.shape, jnp.float32))
    (mean_sum, ref_sum), unused = lax.scan(accumulate, start, (shift_offsets, weights))
    return mean_sum, ref_sum
```

```python
import functools

import jax
import jax.numpy as jnp
from jax import lax
from jax.experimental import pallas as pl
from jax.experimental.pallas import tpu as pltpu
from jax.sharding import PartitionSpec as P

LANES = 128
REACH = 4
SPAN = 2 * REACH + 1
PAD = -3.0e38
BF16 = jnp.bfloat16
F32 = jnp.float32


def split(x):
    hi = x.astype(BF16)
    return hi, (x - hi.astype(F32)).astype(BF16)


def lane_iota(shape):
    return lax.broadcasted_iota(jnp.int32, shape, 1)


def sub_iota(shape):
    return lax.broadcasted_iota(jnp.int32, shape, 0)


def score_body(shifts, offs, scale_ref, group_ref, p_ref, x_ref, out_ref, bank):
    rows = p_ref.shape[1] // LANES
    people = p_ref.shape[0]
    height = rows + 2 * REACH

    def prepare(r, carry):
        x = x_ref[:, pl.ds(pl.multiple_of(r * LANES, LANES), LANES)]
        hi = x.astype(BF16).astype(F32)
        v = jnp.concatenate([hi, x - hi], axis=0)
        for b in range(SPAN):
            turned = pltpu.roll(v, (b - REACH) % LANES, 1) if b != REACH else v
            bank[b * height + r + REACH] = jnp.concatenate([turned, turned], axis=0).astype(BF16)
        return carry

    lax.fori_loop(0, rows, prepare, 0, unroll=2)
    for b in range(SPAN):
        base = b * height
        bank[base : base + REACH] = bank[base + rows : base + rows + REACH]
        bank[base + rows + REACH : base + height] = bank[base + REACH : base + 2 * REACH]

    start = [
        (offs[t, 1] + REACH) * height + REACH - offs[t, 0] for t in range(shifts)
    ]
    lower = sub_iota((16, LANES)) < 8
    pairs = (shifts + 1) // 2

    def step(j, acc):
        y = j * 2
        pieces = []
        for q in range(pairs):
            first = start[2 * q] + y
            second = start[min(2 * q + 1, shifts - 1)] + y
            pieces.append(
                jnp.concatenate(
                    [
                        jnp.where(lower, bank[first + e], bank[second + e])
                        for e in range(2)
                    ],
                    axis=1,
                )
            )
        lhs = jnp.concatenate(pieces, axis=0)
        hi, lo = split(p_ref[:, pl.ds(pl.multiple_of(y * LANES, 2 * LANES), 2 * LANES)])
        rhs = jnp.concatenate([hi, lo, hi, lo], axis=0)
        return acc + lax.dot_general(
            lhs, rhs, (((1,), (1,)), ((), ())), preferred_element_type=F32
        )

    acc = lax.fori_loop(0, rows // 2, step, jnp.zeros((pairs * 16, LANES), F32))

    group = jnp.concatenate([group_ref[...]] * (LANES // people), axis=1)
    scale = jnp.zeros(group.shape, F32)
    for g in range(scale_ref.shape[0]):
        scale = jnp.where(group == g, scale_ref[g], scale)
    scale = scale / rows
    full = []
    for t in range(shifts):
        v = acc[8 * t : 8 * t + 8]
        v = v + pltpu.roll(v, 4, 0)
        full.append((v + pltpu.roll(v, people, 1)) * scale)
    lane_group = lane_iota((8, LANES)) // people
    top = sub_iota((8, LANES)) < 4
    for u in range(4):
        v = jnp.full((8, LANES), PAD, F32)
        for tg in range(LANES // people):
            for h in range(2):
                t = tg * 8 + 2 * u + h
                if t < shifts:
                    here = (lane_group == tg) & (top if h == 0 else ~top)
                    v = jnp.where(here, full[t], v)
        out_ref[8 * u : 8 * u + 8] = v


def score_call(particles, references, offsets, group, scale):
    shifts = offsets.shape[0]
    rows = particles.shape[1] // LANES
    height = rows + 2 * REACH
    vmem = pl.BlockSpec(memory_space=pltpu.VMEM)
    smem = pl.BlockSpec(memory_space=pltpu.SMEM)
    return pl.pallas_call(
        functools.partial(score_body, shifts),
        out_shape=jax.ShapeDtypeStruct((32, LANES), F32),
        in_specs=[smem, smem, vmem, vmem, vmem],
        out_specs=vmem,
        scratch_shapes=[pltpu.VMEM((SPAN * height, 16, LANES), BF16)],
        compiler_params=pltpu.CompilerParams(vmem_limit_bytes=20 << 20),
        cost_estimate=pl.CostEstimate(flops=10**9, bytes_accessed=10**7, transcendentals=0),
        name="scores",
    )(offsets, scale, group, particles, references)


def bank_body(x_ref, out_ref):
    for r in range(x_ref.shape[1] // LANES):
        x = x_ref[:, r * LANES : (r + 1) * LANES]
        for b in range(SPAN):
            turned = pltpu.roll(x, (b - REACH) % LANES, 1) if b != REACH else x
            hi, lo = split(turned)
            out_ref[0, b, r] = jnp.concatenate([hi, lo], axis=0)


def bank_call(slab):
    many, width = slab.shape
    groups, rows = many // 32, width // LANES
    return pl.pallas_call(
        bank_body,
        grid=(groups,),
        out_shape=jax.ShapeDtypeStruct((groups, SPAN, rows, 64, LANES), BF16),
        in_specs=[pl.BlockSpec((32, width), lambda g: (g, 0))],
        out_specs=pl.BlockSpec((1, SPAN, rows, 64, LANES), lambda g: (g, 0, 0, 0, 0)),
        compiler_params=pltpu.CompilerParams(vmem_limit_bytes=20 << 20),
        cost_estimate=pl.CostEstimate(flops=10**9, bytes_accessed=10**7, transcendentals=0),
        name="bank",
    )(slab)


def sums_body(shifts, offs, part, s_ref, p_ref, lhs_ref, keep_ref, send_ref, weights, q_ref):
    count = s_ref.shape[0]
    people = p_ref.shape[0]
    rows = p_ref.shape[1] // LANES
    half = rows // 2
    height = half + 2 * REACH
    folds = LANES // people

    def across(v, combine):
        shift = people
        while shift < LANES:
            v = combine(v, pltpu.roll(v, shift, 1))
            shift *= 2
        return v

    top = lax.fori_loop(
        1, count, lambda m, v: jnp.maximum(v, s_ref[m]), s_ref[0]
    )
    peak = across(jnp.broadcast_to(jnp.max(top, axis=0, keepdims=True), (8, LANES)), jnp.maximum)
    peak = jnp.concatenate([peak] * 4, axis=0)

    def exponent(m, total):
        e = jnp.exp(s_ref[m] - peak)
        weights[m] = e
        return total + e

    total = lax.fori_loop(0, count, exponent, jnp.zeros((32, LANES), F32))
    total = across(
        jnp.broadcast_to(jnp.sum(total, axis=0, keepdims=True), (8, LANES)), jnp.add
    )
    total = jnp.concatenate([total] * 4, axis=0)

    def normalise(m, carry):
        weights[m] = weights[m] / total
        return carry

    lax.fori_loop(0, count, normalise, 0)

    upper = sub_iota((8, LANES)) < 4
    for g in range(count // 8):
        blocks = []
        for tl in range(8):
            u = tl // 2
            for pair in range(4):
                even = weights[8 * g + 2 * pair, 8 * u : 8 * u + 8]
                odd = weights[8 * g + 2 * pair + 1, 8 * u : 8 * u + 8]
                if tl % 2 == 0:
                    odd = pltpu.roll(odd, 4, 0)
                else:
                    even = pltpu.roll(even, 4, 0)
                blocks.append(jnp.where(upper, even, odd))
        turned = jnp.transpose(jnp.concatenate(blocks, axis=0))
        left = jnp.concatenate(
            [turned[people * tg : people * (tg + 1)] for tg in range(folds)], axis=1
        )[:, : shifts * 32]
        hi, lo = split(left)
        lhs_ref[g] = jnp.concatenate([hi, lo], axis=0)

    lane_group = lane_iota((8, LANES)) // people
    lefts = []
    for t in range(shifts):
        tg, tl = t // 8, t % 8
        v = weights[0, 8 * (tl // 2) : 8 * (tl // 2) + 8]
        v = across(jnp.where(lane_group == tg, v, 0.0), jnp.add)
        other = pltpu.roll(v, 4, 0)
        v = jnp.where(upper, v, other) if tl % 2 == 0 else jnp.where(upper, other, v)
        hi = v.astype(BF16).astype(F32)
        v = jnp.where(lane_group < folds // 2, hi, v - hi)
        zero = jnp.zeros_like(v)
        lefts.append(
            jnp.concatenate([jnp.where(upper, v, zero), jnp.where(upper, zero, v)], axis=1)
        )
    left = jnp.concatenate(lefts, axis=0).astype(BF16)

    def product(j, carry):
        rights = []
        for h in range(2):
            y = lax.rem(2 * j + h * half + rows - REACH, rows)
            hi, lo = split(p_ref[:, pl.ds(pl.multiple_of(y * LANES, 2 * LANES), 2 * LANES)])
            rights += [hi, lo, hi, lo]
        out = jnp.dot(left, jnp.concatenate(rights, axis=0), preferred_element_type=F32)
        for t in range(shifts):
            for e in range(2):
                q_ref[t * height + 2 * j + e] = out[8 * t : 8 * t + 8, e * LANES : (e + 1) * LANES]
        return carry

    lax.fori_loop(0, height // 2, product, 0)

    start = [t * height + REACH + offs[t, 0] for t in range(shifts)]
    turn = [lax.rem(LANES - offs[t, 1], LANES) for t in range(shifts)]
    swap = part[0] == 1

    def gather(y, carry):
        acc = pltpu.roll(q_ref[start[0] + y], turn[0], 1)
        for t in range(1, shifts):
            acc = acc + pltpu.roll(q_ref[start[t] + y], turn[t], 1)
        acc = jnp.where(swap, pltpu.roll(acc, 4, 0), acc)
        at = pl.ds(pl.multiple_of(y * LANES, LANES), LANES)
        keep_ref[:, at] = acc[:4]
        send_ref[:, at] = acc[4:]
        return carry

    lax.fori_loop(0, half, gather, 0)


def sums_call(scores, particles, offsets, part):
    shifts = offsets.shape[0]
    count = scores.shape[0]
    pixels = particles.shape[1]
    height = pixels // LANES // 2 + 2 * REACH
    vmem = pl.BlockSpec(memory_space=pltpu.VMEM)
    smem = pl.BlockSpec(memory_space=pltpu.SMEM)
    return pl.pallas_call(
        functools.partial(sums_body, shifts),
        out_shape=(
            jax.ShapeDtypeStruct((count // 8, 64, shifts * 32), BF16),
            jax.ShapeDtypeStruct((4, pixels // 2), F32),
            jax.ShapeDtypeStruct((4, pixels // 2), F32),
        ),
        in_specs=[smem, smem, vmem, vmem],
        out_specs=(vmem, vmem, vmem),
        scratch_shapes=[
            pltpu.VMEM((count, 32, LANES), F32),
            pltpu.VMEM((shifts * height, 8, LANES), F32),
        ],
        compiler_params=pltpu.CompilerParams(vmem_limit_bytes=24 << 20),
        cost_estimate=pl.CostEstimate(flops=10**9, bytes_accessed=10**7, transcendentals=10**5),
        name="sums",
    )(offsets, part, scores, particles)


def mean_body(shifts, offs, lhs_ref, bank_ref, out_ref):
    rows = out_ref.shape[1] // LANES
    step_rows = 2 if rows % 2 == 0 else 1
    people = out_ref.shape[0]
    lefts = lhs_ref[0]

    @pl.when(pl.program_id(0) == 0)
    def _():
        out_ref[...] = jnp.zeros_like(out_ref)

    def step(j, carry):
        y = j * step_rows
        his, los = [], []
        for t in range(shifts):
            b = offs[t, 1] + REACH
            r = y + REACH - offs[t, 0]
            tiles = [bank_ref[0, b, r + e] for e in range(step_rows)]
            tile = jnp.concatenate(tiles, axis=1) if step_rows > 1 else tiles[0]
            his.append(tile[:32])
            los.append(tile[32:])
        both = jnp.dot(lefts, jnp.concatenate(his, axis=0), preferred_element_type=F32)
        rest = jnp.dot(lefts[:people], jnp.concatenate(los, axis=0), preferred_element_type=F32)
        at = pl.ds(pl.multiple_of(y * LANES, step_rows * LANES), step_rows * LANES)
        out_ref[:, at] += both[:people] + both[people:] + rest
        return carry

    lax.fori_loop(0, rows // step_rows, step, 0)


def mean_call(lefts, bank, offsets, people):
    shifts = offsets.shape[0]
    groups, span, tall, wide, lanes = bank.shape
    width = (tall - 2 * REACH) * LANES
    smem = pl.BlockSpec(memory_space=pltpu.SMEM)
    return pl.pallas_call(
        functools.partial(mean_body, shifts),
        grid=(groups,),
        out_shape=jax.ShapeDtypeStruct((people, width), F32),
        in_specs=[
            smem,
            pl.BlockSpec((1,) + lefts.shape[1:], lambda g: (g, 0, 0)),
            pl.BlockSpec((1, span, tall, wide, lanes), lambda g: (g, 0, 0, 0, 0)),
        ],
        out_specs=pl.BlockSpec((people, width), lambda g: (0, 0)),
        compiler_params=pltpu.CompilerParams(vmem_limit_bytes=20 << 20),
        cost_estimate=pl.CostEstimate(flops=10**9, bytes_accessed=10**7, transcendentals=0),
        name="mean",
    )(offsets, lefts, bank)


def local(particles, references, shift_offsets, particle_group, group_scale):
    people, pixels = particles.shape
    count = lax.axis_size("refs")
    rows = pixels // LANES
    own = rows // count
    assert references.shape[0] == 4 and people * 4 == LANES and count % 8 == 0
    assert shift_offsets.shape[0] <= 32 and lax.axis_size("parts") == 2
    me = lax.axis_index("refs")
    bits = []
    d = count // 2
    while d:
        bits.append(d)
        d //= 2

    def swap(value, d):
        return lax.ppermute(value, "refs", [(i, i ^ d) for i in range(count)])

    slab = jnp.concatenate(
        [references[:, -REACH * LANES :], references, references[:, : REACH * LANES]], axis=1
    )
    for d in bits:
        side = (me // d) % 2
        wide = (d * own + 2 * REACH) * LANES
        jump = d * own * LANES
        keep = lax.dynamic_slice_in_dim(slab, side * jump, wide, 1)
        send = lax.dynamic_slice_in_dim(slab, (1 - side) * jump, wide, 1)
        slab = jnp.concatenate([keep, swap(send, d)], axis=0)
    bank = bank_call(slab)

    scores = score_call(
        particles, references, shift_offsets, particle_group.reshape(1, people), group_scale
    )[None]
    for d in bits:
        scores = jnp.concatenate([scores, swap(scores, d)], axis=0)

    part = lax.axis_index("parts").reshape(1).astype(jnp.int32)
    lefts, keep, send = sums_call(scores, particles, shift_offsets, part)
    other = lax.ppermute(send, "parts", [(0, 1), (1, 0)])
    posterior_mean = mean_call(lefts, bank, shift_offsets, people)
    return posterior_mean, keep + other


def solution(mesh):
    return jax.shard_map(
        local,
        mesh=mesh,
        in_specs=(
            P(("groups", "parts"), None),
            P(("groups", "refs"), None),
            P("groups", None),
            P(("groups", "parts")),
            P(),
        ),
        out_specs=(P(("groups", "parts"), "refs"), P(("groups", "refs"), "parts")),
        check_vma=False,
    )
```

```python
import functools

import jax
import jax.numpy as jnp
from jax import lax
from jax.experimental import pallas as pl
from jax.experimental.pallas import tpu as pltpu
from jax.sharding import PartitionSpec as P


LANES = 128
REACH = 4
SPAN = 2 * REACH + 1
PAD = -3.0e38
BF16 = jnp.bfloat16
F32 = jnp.float32


def split(x):
    hi = x.astype(BF16)
    return hi, (x - hi.astype(F32)).astype(BF16)


def lane_iota(shape):
    return lax.broadcasted_iota(jnp.int32, shape, 1)


def sub_iota(shape):
    return lax.broadcasted_iota(jnp.int32, shape, 0)


def score_body(
    shifts, offs_hbm, scale_hbm, group_hbm, p_ref, x_ref, out_ref, bank, offs, scale_ref, group_ref, sems
):
    rows = p_ref.shape[1] // LANES
    people = p_ref.shape[0]
    height = rows + 2 * REACH
    copies = [
        pltpu.make_async_copy(offs_hbm, offs, sems.at[0]),
        pltpu.make_async_copy(scale_hbm, scale_ref, sems.at[1]),
        pltpu.make_async_copy(group_hbm, group_ref, sems.at[2]),
    ]
    for copy in copies:
        copy.start()

    def prepare(r, carry):
        x = x_ref[:, pl.ds(pl.multiple_of(r * LANES, LANES), LANES)]
        hi = x.astype(BF16).astype(F32)
        v = jnp.concatenate([hi, x - hi], axis=0)
        for b in range(SPAN):
            turned = pltpu.roll(v, (b - REACH) % LANES, 1) if b != REACH else v
            bank[b * height + r + REACH] = jnp.concatenate([turned, turned], axis=0).astype(BF16)
        return carry

    lax.fori_loop(0, rows, prepare, 0, unroll=32)
    for b in range(SPAN):
        base = b * height
        bank[base : base + REACH] = bank[base + rows : base + rows + REACH]
        bank[base + rows + REACH : base + height] = bank[base + REACH : base + 2 * REACH]

    for copy in copies:
        copy.wait()
    start = [
        (offs[1, t] + REACH) * height + REACH - offs[0, t] for t in range(shifts)
    ]
    lower = sub_iota((16, LANES)) < 8
    pairs = (shifts + 1) // 2
    deep = 32

    def step(j, acc):
        y = j * deep
        pieces = []
        for q in range(pairs):
            first = start[2 * q] + y
            second = start[min(2 * q + 1, shifts - 1)] + y
            pieces.append(
                jnp.concatenate(
                    [
                        jnp.where(lower, bank[first + e], bank[second + e])
                        for e in range(deep)
                    ],
                    axis=1,
                )
            )
        lhs = jnp.concatenate(pieces, axis=0)
        at = pl.ds(pl.multiple_of(y * LANES, deep * LANES), deep * LANES)
        rhs = jnp.concatenate(split(p_ref[:, at]), axis=0)
        return acc + lax.dot_general(
            lhs, rhs, (((1,), (1,)), ((), ())), preferred_element_type=F32
        )

    acc = lax.fori_loop(0, rows // deep, step, jnp.zeros((pairs * 16, 2 * people), F32))
    acc = jnp.concatenate([acc] * (LANES // (2 * people)), axis=1)

    group = jnp.concatenate([group_ref[...]] * (LANES // people), axis=1)
    scale = jnp.zeros(group.shape, F32)
    for g in range(scale_ref.shape[0]):
        scale = jnp.where(group == g, scale_ref[g], scale)
    scale = scale / rows
    full = []
    for t in range(shifts):
        v = acc[8 * t : 8 * t + 8]
        v = v + pltpu.roll(v, 4, 0)
        full.append((v + pltpu.roll(v, people, 1)) * scale)
    lane_group = lane_iota((8, LANES)) // people
    top = sub_iota((8, LANES)) < 4
    for u in range(4):
        v = jnp.full((8, LANES), PAD, F32)
        for tg in range(LANES // people):
            for h in range(2):
                t = tg * 8 + 2 * u + h
                if t < shifts:
                    here = (lane_group == tg) & (top if h == 0 else ~top)
                    v = jnp.where(here, full[t], v)
        out_ref[8 * u : 8 * u + 8] = v


def score_call(particles, references, offsets, group, scale):
    shifts = offsets.shape[1]
    rows = particles.shape[1] // LANES
    height = rows + 2 * REACH
    vmem = pl.BlockSpec(memory_space=pltpu.VMEM)
    hbm = pl.BlockSpec(memory_space=pltpu.HBM)
    return pl.pallas_call(
        functools.partial(score_body, shifts),
        out_shape=jax.ShapeDtypeStruct((32, LANES), F32),
        in_specs=[hbm, hbm, hbm, vmem, vmem],
        out_specs=vmem,
        scratch_shapes=[
            pltpu.VMEM((SPAN * height, 16, LANES), BF16),
            pltpu.SMEM(offsets.shape, jnp.int32),
            pltpu.SMEM(scale.shape, F32),
            pltpu.VMEM(group.shape, jnp.int32),
            pltpu.SemaphoreType.DMA((3,)),
        ],
        compiler_params=pltpu.CompilerParams(vmem_limit_bytes=20 << 20),
        cost_estimate=pl.CostEstimate(flops=10**9, bytes_accessed=10**7, transcendentals=0),
        name="scores",
    )(offsets, scale, group, particles, references)


def bank_body(x_ref, out_ref):
    for r in range(x_ref.shape[1] // LANES):
        x = x_ref[:, r * LANES : (r + 1) * LANES]
        for b in range(SPAN):
            turned = pltpu.roll(x, (b - REACH) % LANES, 1) if b != REACH else x
            hi, lo = split(turned)
            out_ref[0, b, r] = jnp.concatenate([hi, lo], axis=0)


def bank_call(slab):
    many, width = slab.shape
    groups, rows = many // 32, width // LANES
    return pl.pallas_call(
        bank_body,
        grid=(groups,),
        out_shape=jax.ShapeDtypeStruct((groups, SPAN, rows, 64, LANES), BF16),
        in_specs=[pl.BlockSpec((32, width), lambda g: (g, 0))],
        out_specs=pl.BlockSpec((1, SPAN, rows, 64, LANES), lambda g: (g, 0, 0, 0, 0)),
        compiler_params=pltpu.CompilerParams(vmem_limit_bytes=20 << 20),
        cost_estimate=pl.CostEstimate(flops=10**9, bytes_accessed=10**7, transcendentals=0),
        name="bank",
    )(slab)


def sums_body(
    shifts, places, offs_hbm, part, s_ref, p_ref, lhs_ref, keep_ref, send_ref, weights, q_ref, offs, sem
):
    count = s_ref.shape[0]
    people = p_ref.shape[0]
    rows = p_ref.shape[1] // LANES
    half = rows // 2
    height = half + 2 * REACH
    folds = LANES // people
    copy = pltpu.make_async_copy(offs_hbm, offs, sem)
    copy.start()

    def across(v, combine):
        shift = people
        while shift < LANES:
            v = combine(v, pltpu.roll(v, shift, 1))
            shift *= 2
        return v

    top = lax.fori_loop(
        1, count, lambda m, v: jnp.maximum(v, s_ref[m]), s_ref[0]
    )
    peak = across(jnp.broadcast_to(jnp.max(top, axis=0, keepdims=True), (8, LANES)), jnp.maximum)
    peak = jnp.concatenate([peak] * 4, axis=0)

    def exponent(m, total):
        e = jnp.exp(s_ref[m] - peak)
        weights[m] = e
        return total + e

    total = lax.fori_loop(0, count, exponent, jnp.zeros((32, LANES), F32))
    total = across(
        jnp.broadcast_to(jnp.sum(total, axis=0, keepdims=True), (8, LANES)), jnp.add
    )
    total = jnp.concatenate([total] * 4, axis=0)

    def normalise(m, carry):
        weights[m] = weights[m] / total
        return carry

    lax.fori_loop(0, count, normalise, 0)

    upper = sub_iota((8, LANES)) < 4
    for g in range(count // 8):
        blocks = []
        for tl in range(8):
            u = tl // 2
            for pair in range(4):
                first, second = places[8 * g + 2 * pair], places[8 * g + 2 * pair + 1]
                even = weights[first, 8 * u : 8 * u + 8]
                odd = weights[second, 8 * u : 8 * u + 8]
                if tl % 2 == 0:
                    odd = pltpu.roll(odd, 4, 0)
                else:
                    even = pltpu.roll(even, 4, 0)
                blocks.append(jnp.where(upper, even, odd))
        turned = jnp.transpose(jnp.concatenate(blocks, axis=0))
        left = jnp.concatenate(
            [turned[people * tg : people * (tg + 1)] for tg in range(folds)], axis=1
        )[:, : shifts * 32]
        hi, lo = split(left)
        lhs_ref[g] = jnp.concatenate([hi, lo], axis=0)

    lane_group = lane_iota((8, LANES)) // people
    lefts = []
    for t in range(shifts):
        tg, tl = t // 8, t % 8
        v = weights[0, 8 * (tl // 2) : 8 * (tl // 2) + 8]
        v = across(jnp.where(lane_group == tg, v, 0.0), jnp.add)
        other = pltpu.roll(v, 4, 0)
        v = jnp.where(upper, v, other) if tl % 2 == 0 else jnp.where(upper, other, v)
        hi = v.astype(BF16).astype(F32)
        v = jnp.where(lane_group < folds // 2, hi, v - hi)
        zero = jnp.zeros_like(v)
        lefts.append(
            jnp.concatenate([jnp.where(upper, v, zero), jnp.where(upper, zero, v)], axis=1)
        )
    left = jnp.concatenate(lefts, axis=0).astype(BF16)

    def product(j, carry):
        rights = []
        for h in range(2):
            y = lax.rem(2 * j + h * half + rows - REACH, rows)
            hi, lo = split(p_ref[:, pl.ds(pl.multiple_of(y * LANES, 2 * LANES), 2 * LANES)])
            rights += [hi, lo, hi, lo]
        out = jnp.dot(left, jnp.concatenate(rights, axis=0), preferred_element_type=F32)
        for t in range(shifts):
            for e in range(2):
                q_ref[t * height + 2 * j + e] = out[8 * t : 8 * t + 8, e * LANES : (e + 1) * LANES]
        return carry

    lax.fori_loop(0, height // 2, product, 0, unroll=12)
    copy.wait()

    start = [t * height + REACH + offs[0, t] for t in range(shifts)]
    turn = [lax.rem(LANES - offs[1, t], LANES) for t in range(shifts)]
    swap = part[0] == 1

    def gather(y, carry):
        acc = pltpu.roll(q_ref[start[0] + y], turn[0], 1)
        for t in range(1, shifts):
            acc = acc + pltpu.roll(q_ref[start[t] + y], turn[t], 1)
        acc = jnp.where(swap, pltpu.roll(acc, 4, 0), acc)
        at = pl.ds(pl.multiple_of(y * LANES, LANES), LANES)
        keep_ref[:, at] = acc[:4]
        send_ref[:, at] = acc[4:]
        return carry

    lax.fori_loop(0, half, gather, 0, unroll=16)


def sums_call(places, scores, particles, offsets, part):
    shifts = offsets.shape[1]
    count = scores.shape[0]
    pixels = particles.shape[1]
    height = pixels // LANES // 2 + 2 * REACH
    vmem = pl.BlockSpec(memory_space=pltpu.VMEM)
    smem = pl.BlockSpec(memory_space=pltpu.SMEM)
    hbm = pl.BlockSpec(memory_space=pltpu.HBM)
    return pl.pallas_call(
        functools.partial(sums_body, shifts, places),
        out_shape=(
            jax.ShapeDtypeStruct((count // 8, 64, shifts * 32), BF16),
            jax.ShapeDtypeStruct((4, pixels // 2), F32),
            jax.ShapeDtypeStruct((4, pixels // 2), F32),
        ),
        in_specs=[hbm, smem, vmem, vmem],
        out_specs=(vmem, vmem, vmem),
        scratch_shapes=[
            pltpu.VMEM((count, 32, LANES), F32),
            pltpu.VMEM((shifts * height, 8, LANES), F32),
            pltpu.SMEM(offsets.shape, jnp.int32),
            pltpu.SemaphoreType.DMA,
        ],
        compiler_params=pltpu.CompilerParams(vmem_limit_bytes=24 << 20),
        cost_estimate=pl.CostEstimate(flops=10**9, bytes_accessed=10**7, transcendentals=10**5),
        name="sums",
    )(offsets, part, scores, particles)


def mean_body(shifts, offs, lhs_ref, bank_ref, out_ref):
    rows = out_ref.shape[1] // LANES
    step_rows = 2 if rows % 2 == 0 else 1
    people = out_ref.shape[0]
    lefts = lhs_ref[0]

    @pl.when(pl.program_id(0) == 0)
    def _():
        out_ref[...] = jnp.zeros_like(out_ref)

    def step(j, carry):
        y = j * step_rows
        his, los = [], []
        for t in range(shifts):
            b = offs[1, t] + REACH
            r = y + REACH - offs[0, t]
            tiles = [bank_ref[0, b, r + e] for e in range(step_rows)]
            tile = jnp.concatenate(tiles, axis=1) if step_rows > 1 else tiles[0]
            his.append(tile[:32])
            los.append(tile[32:])
        both = jnp.dot(lefts, jnp.concatenate(his, axis=0), preferred_element_type=F32)
        rest = jnp.dot(lefts[:people], jnp.concatenate(los, axis=0), preferred_element_type=F32)
        at = pl.ds(pl.multiple_of(y * LANES, step_rows * LANES), step_rows * LANES)
        out_ref[:, at] += both[:people] + both[people:] + rest
        return carry

    lax.fori_loop(0, rows // step_rows, step, 0, unroll=min(8, rows // step_rows))


def mean_call(lefts, bank, offsets, people):
    shifts = offsets.shape[1]
    groups, span, tall, wide, lanes = bank.shape
    width = (tall - 2 * REACH) * LANES
    smem = pl.BlockSpec(memory_space=pltpu.SMEM)
    return pl.pallas_call(
        functools.partial(mean_body, shifts),
        grid=(groups,),
        out_shape=jax.ShapeDtypeStruct((people, width), F32),
        in_specs=[
            smem,
            pl.BlockSpec((1,) + lefts.shape[1:], lambda g: (g, 0, 0)),
            pl.BlockSpec((1, span, tall, wide, lanes), lambda g: (g, 0, 0, 0, 0)),
        ],
        out_specs=pl.BlockSpec((people, width), lambda g: (0, 0)),
        compiler_params=pltpu.CompilerParams(vmem_limit_bytes=20 << 20),
        cost_estimate=pl.CostEstimate(flops=10**9, bytes_accessed=10**7, transcendentals=0),
        name="mean",
    )(offsets, lefts, bank)


def local(particles, references, shift_offsets, particle_group, group_scale):
    people, pixels = particles.shape
    count = lax.axis_size("refs")
    rows = pixels // LANES
    own = rows // count
    assert references.shape[0] == 4 and people * 4 == LANES and count % 8 == 0
    assert shift_offsets.shape[0] <= 32 and lax.axis_size("parts") == 2
    me = lax.axis_index("refs")
    offsets = shift_offsets.T
    bits = []
    d = count // 2
    while d:
        bits.append(d)
        d //= 2

    def swap(value, d):
        return lax.ppermute(value, "refs", [(i, i ^ d) for i in range(count)])

    slab = jnp.concatenate(
        [references[:, -REACH * LANES :], references, references[:, : REACH * LANES]], axis=1
    )
    slab_order = [0]
    for d in bits:
        side = (me // d) % 2
        wide = (d * own + 2 * REACH) * LANES
        jump = d * own * LANES
        keep = lax.dynamic_slice_in_dim(slab, side * jump, wide, 1)
        send = lax.dynamic_slice_in_dim(slab, (1 - side) * jump, wide, 1)
        slab = jnp.concatenate([keep, swap(send, d)], axis=0)
        slab_order += [m ^ d for m in slab_order]
    bank = bank_call(slab)

    scores = score_call(
        particles, references, offsets, particle_group.reshape(1, people), group_scale
    )[None]
    order = [0]
    for d in bits[-1:] + bits[:-1]:
        scores = jnp.concatenate([scores, swap(scores, d)], axis=0)
        order += [m ^ d for m in order]
    places = [order.index(m) for m in slab_order]

    part = lax.axis_index("parts").reshape(1).astype(jnp.int32)
    lefts, keep, send = sums_call(places, scores, particles, offsets, part)
    other = lax.ppermute(send, "parts", [(0, 1), (1, 0)])
    posterior_mean = mean_call(lefts, bank, offsets, people)
    return posterior_mean, keep + other


def solution(mesh):
    return jax.shard_map(
        local,
        mesh=mesh,
        in_specs=(
            P(("groups", "parts"), None),
            P(("groups", "refs"), None),
            P("groups", None),
            P(("groups", "parts")),
            P(),
        ),
        out_specs=(P(("groups", "parts"), "refs"), P(("groups", "refs"), "parts")),
        check_vma=False,
    )
```

```python
import functools

import jax
import jax.numpy as jnp
from jax import lax
from jax.experimental import pallas as pl
from jax.experimental.pallas import tpu as pltpu
from jax.sharding import PartitionSpec as P


LANES = 128
REACH = 4
SPAN = 2 * REACH + 1
PAD = -3.0e38
BF16 = jnp.bfloat16
F32 = jnp.float32


def split(x):
    hi = x.astype(BF16)
    return hi, (x - hi.astype(F32)).astype(BF16)


def lane_iota(shape):
    return lax.broadcasted_iota(jnp.int32, shape, 1)


def sub_iota(shape):
    return lax.broadcasted_iota(jnp.int32, shape, 0)


def front_body(d, own, x_ref, keep_ref, send_ref):
    width = x_ref.shape[1]
    side = (lax.axis_index("refs") // d) % 2
    jump, halo = d * own * LANES, REACH * LANES
    for out, which in ((keep_ref, side), (send_ref, 1 - side)):
        middle = which * jump
        before = lax.rem(middle + width - halo, width)
        after = lax.rem(middle + jump, width)
        out[:, :halo] = x_ref[:, pl.ds(pl.multiple_of(before, LANES), halo)]
        out[:, halo : halo + jump] = x_ref[:, pl.ds(pl.multiple_of(middle, LANES), jump)]
        out[:, halo + jump :] = x_ref[:, pl.ds(pl.multiple_of(after, LANES), halo)]


def front_call(references, d, own):
    wide = (d * own + 2 * REACH) * LANES
    vmem = pl.BlockSpec(memory_space=pltpu.VMEM)
    shape = jax.ShapeDtypeStruct((references.shape[0], wide), F32)
    return pl.pallas_call(
        functools.partial(front_body, d, own),
        out_shape=(shape, shape),
        in_specs=[vmem],
        out_specs=(vmem, vmem),
        compiler_params=pltpu.CompilerParams(vmem_limit_bytes=4 << 20),
        cost_estimate=pl.CostEstimate(flops=8 * 10**9, bytes_accessed=10**7, transcendentals=0),
        name="front",
    )(references)


def score_body(
    shifts, offs_hbm, p_ref, x_ref, out_ref, bank, offs, sem
):
    rows = p_ref.shape[1] // LANES
    people = p_ref.shape[0]
    height = rows + 2 * REACH
    copy = pltpu.make_async_copy(offs_hbm, offs, sem)
    copy.start()

    def prepare(r, carry):
        x = x_ref[:, pl.ds(pl.multiple_of(r * LANES, LANES), LANES)]
        hi = x.astype(BF16).astype(F32)
        v = jnp.concatenate([hi, x - hi], axis=0)
        for b in range(SPAN):
            turned = pltpu.roll(v, (b - REACH) % LANES, 1) if b != REACH else v
            bank[b * height + r + REACH] = jnp.concatenate([turned, turned], axis=0).astype(BF16)
        return carry

    lax.fori_loop(0, rows, prepare, 0, unroll=32)
    for b in range(SPAN):
        base = b * height
        bank[base : base + REACH] = bank[base + rows : base + rows + REACH]
        bank[base + rows + REACH : base + height] = bank[base + REACH : base + 2 * REACH]

    copy.wait()
    start = [
        (offs[1, t] + REACH) * height + REACH - offs[0, t] for t in range(shifts)
    ]
    lower = sub_iota((16, LANES)) < 8
    pairs = (shifts + 1) // 2
    deep = 32

    def step(j, acc):
        y = j * deep
        pieces = []
        for q in range(pairs):
            first = start[2 * q] + y
            second = start[min(2 * q + 1, shifts - 1)] + y
            pieces.append(
                jnp.concatenate(
                    [
                        jnp.where(lower, bank[first + e], bank[second + e])
                        for e in range(deep)
                    ],
                    axis=1,
                )
            )
        lhs = jnp.concatenate(pieces, axis=0)
        at = pl.ds(pl.multiple_of(y * LANES, deep * LANES), deep * LANES)
        rhs = jnp.concatenate(split(p_ref[:, at]), axis=0)
        return acc + lax.dot_general(
            lhs, rhs, (((1,), (1,)), ((), ())), preferred_element_type=F32
        )

    acc = lax.fori_loop(0, rows // deep, step, jnp.zeros((pairs * 16, 2 * people), F32))
    acc = jnp.concatenate([acc] * (LANES // (2 * people)), axis=1)

    full = []
    for t in range(shifts):
        v = acc[8 * t : 8 * t + 8]
        v = v + pltpu.roll(v, 4, 0)
        full.append(v + pltpu.roll(v, people, 1))
    lane_group = lane_iota((8, LANES)) // people
    top = sub_iota((8, LANES)) < 4
    for u in range(4):
        v = jnp.full((8, LANES), PAD, F32)
        for tg in range(LANES // people):
            for h in range(2):
                t = tg * 8 + 2 * u + h
                if t < shifts:
                    here = (lane_group == tg) & (top if h == 0 else ~top)
                    v = jnp.where(here, full[t], v)
        out_ref[8 * u : 8 * u + 8] = v


def score_call(particles, references, offsets):
    shifts = offsets.shape[1]
    rows = particles.shape[1] // LANES
    height = rows + 2 * REACH
    vmem = pl.BlockSpec(memory_space=pltpu.VMEM)
    hbm = pl.BlockSpec(memory_space=pltpu.HBM)
    return pl.pallas_call(
        functools.partial(score_body, shifts),
        out_shape=jax.ShapeDtypeStruct((32, LANES), F32),
        in_specs=[hbm, vmem, vmem],
        out_specs=vmem,
        scratch_shapes=[
            pltpu.VMEM((SPAN * height, 16, LANES), BF16),
            pltpu.SMEM(offsets.shape, jnp.int32),
            pltpu.SemaphoreType.DMA,
        ],
        compiler_params=pltpu.CompilerParams(vmem_limit_bytes=20 << 20),
        cost_estimate=pl.CostEstimate(flops=10**9, bytes_accessed=10**7, transcendentals=0),
        name="scores",
    )(offsets, particles, references)


def bank_body(x_ref, out_ref):
    for r in range(x_ref.shape[1] // LANES):
        x = x_ref[:, r * LANES : (r + 1) * LANES]
        for b in range(SPAN):
            turned = pltpu.roll(x, (b - REACH) % LANES, 1) if b != REACH else x
            hi, lo = split(turned)
            out_ref[0, b, r] = jnp.concatenate([hi, lo], axis=0)


def bank_call(slab):
    many, width = slab.shape
    groups, rows = many // 32, width // LANES
    return pl.pallas_call(
        bank_body,
        grid=(groups,),
        out_shape=jax.ShapeDtypeStruct((groups, SPAN, rows, 64, LANES), BF16),
        in_specs=[pl.BlockSpec((32, width), lambda g: (g, 0))],
        out_specs=pl.BlockSpec((1, SPAN, rows, 64, LANES), lambda g: (g, 0, 0, 0, 0)),
        compiler_params=pltpu.CompilerParams(vmem_limit_bytes=20 << 20),
        cost_estimate=pl.CostEstimate(flops=10**9, bytes_accessed=10**7, transcendentals=0),
        name="bank",
    )(slab)


def sums_body(
    shifts,
    places,
    offs_hbm,
    scale_hbm,
    group_ref,
    s_ref,
    p_ref,
    lhs_ref,
    keep_ref,
    send_ref,
    weights,
    q_ref,
    offs,
    scale_ref,
    sems,
):
    count = s_ref.shape[0]
    people = p_ref.shape[0]
    rows = p_ref.shape[1] // LANES
    half = rows // 2
    height = half + 2 * REACH
    folds = LANES // people
    copy = pltpu.make_async_copy(offs_hbm, offs, sems.at[0])
    copy.start()
    scale_copy = pltpu.make_async_copy(scale_hbm, scale_ref, sems.at[1])
    scale_copy.start()

    def across(v, combine):
        shift = people
        while shift < LANES:
            v = combine(v, pltpu.roll(v, shift, 1))
            shift *= 2
        return v

    group = jnp.broadcast_to(
        jnp.concatenate([group_ref[...]] * folds, axis=1), (32, LANES)
    )
    scale_copy.wait()
    scale = jnp.zeros(group.shape, F32)
    for g in range(scale_ref.shape[0]):
        scale = jnp.where(group == g, scale_ref[g], scale)
    scale = scale / rows
    top = lax.fori_loop(
        1, count, lambda m, v: jnp.maximum(v, s_ref[m]), s_ref[0], unroll=8 if count == 8 else 1
    ) * scale
    peak = across(jnp.broadcast_to(jnp.max(top, axis=0, keepdims=True), (8, LANES)), jnp.maximum)
    peak = jnp.concatenate([peak] * 4, axis=0)

    def exponent(m, total):
        e = jnp.exp(s_ref[m] * scale - peak)
        weights[m] = e
        return total + e

    total = lax.fori_loop(0, count, exponent, jnp.zeros((32, LANES), F32), unroll=4)
    total = across(
        jnp.broadcast_to(jnp.sum(total, axis=0, keepdims=True), (8, LANES)), jnp.add
    )
    total = jnp.concatenate([total] * 4, axis=0)

    def normalise(m, carry):
        weights[m] = weights[m] / total
        return carry

    lax.fori_loop(0, count, normalise, 0, unroll=4)

    upper = sub_iota((8, LANES)) < 4
    for g in range(count // 8):
        blocks = []
        for tl in range(8):
            u = tl // 2
            for pair in range(4):
                first, second = places[8 * g + 2 * pair], places[8 * g + 2 * pair + 1]
                even = weights[first, 8 * u : 8 * u + 8]
                odd = weights[second, 8 * u : 8 * u + 8]
                if tl % 2 == 0:
                    odd = pltpu.roll(odd, 4, 0)
                else:
                    even = pltpu.roll(even, 4, 0)
                blocks.append(jnp.where(upper, even, odd))
        turned = jnp.transpose(jnp.concatenate(blocks, axis=0))
        left = jnp.concatenate(
            [turned[people * tg : people * (tg + 1)] for tg in range(folds)], axis=1
        )[:, : shifts * 32]
        hi, lo = split(left)
        lhs_ref[g] = jnp.concatenate([hi, lo], axis=0)

    lane_group = lane_iota((8, LANES)) // people
    lefts = []
    for t in range(shifts):
        tg, tl = t // 8, t % 8
        v = weights[0, 8 * (tl // 2) : 8 * (tl // 2) + 8]
        v = across(jnp.where(lane_group == tg, v, 0.0), jnp.add)
        other = pltpu.roll(v, 4, 0)
        v = jnp.where(upper, v, other) if tl % 2 == 0 else jnp.where(upper, other, v)
        hi = v.astype(BF16).astype(F32)
        v = jnp.where(lane_group < folds // 2, hi, v - hi)
        zero = jnp.zeros_like(v)
        lefts.append(
            jnp.concatenate([jnp.where(upper, v, zero), jnp.where(upper, zero, v)], axis=1)
        )
    left = jnp.concatenate(lefts, axis=0).astype(BF16)

    def product(j, carry):
        rights = []
        for h in range(2):
            y = lax.rem(2 * j + h * half + rows - REACH, rows)
            hi, lo = split(p_ref[:, pl.ds(pl.multiple_of(y * LANES, 2 * LANES), 2 * LANES)])
            rights += [hi, lo, hi, lo]
        out = jnp.dot(left, jnp.concatenate(rights, axis=0), preferred_element_type=F32)
        for t in range(shifts):
            for e in range(2):
                q_ref[t * height + 2 * j + e] = out[8 * t : 8 * t + 8, e * LANES : (e + 1) * LANES]
        return carry

    lax.fori_loop(0, height // 2, product, 0, unroll=12)
    copy.wait()

    start = [t * height + REACH + offs[0, t] for t in range(shifts)]
    turn = [lax.rem(LANES - offs[1, t], LANES) for t in range(shifts)]
    swap = lax.axis_index("parts") == 1

    def gather(y, carry):
        acc = pltpu.roll(q_ref[start[0] + y], turn[0], 1)
        for t in range(1, shifts):
            acc = acc + pltpu.roll(q_ref[start[t] + y], turn[t], 1)
        acc = jnp.where(swap, pltpu.roll(acc, 4, 0), acc)
        at = pl.ds(pl.multiple_of(y * LANES, LANES), LANES)
        keep_ref[:, at] = acc[:4]
        send_ref[:, at] = acc[4:]
        return carry

    lax.fori_loop(0, half, gather, 0, unroll=16)


def sums_call(places, scores, particles, offsets, group, scale):
    shifts = offsets.shape[1]
    count = scores.shape[0]
    pixels = particles.shape[1]
    height = pixels // LANES // 2 + 2 * REACH
    vmem = pl.BlockSpec(memory_space=pltpu.VMEM)
    hbm = pl.BlockSpec(memory_space=pltpu.HBM)
    return pl.pallas_call(
        functools.partial(sums_body, shifts, places),
        out_shape=(
            jax.ShapeDtypeStruct((count // 8, 64, shifts * 32), BF16),
            jax.ShapeDtypeStruct((4, pixels // 2), F32),
            jax.ShapeDtypeStruct((4, pixels // 2), F32),
        ),
        in_specs=[hbm, hbm, vmem, vmem, vmem],
        out_specs=(vmem, vmem, vmem),
        scratch_shapes=[
            pltpu.VMEM((count, 32, LANES), F32),
            pltpu.VMEM((shifts * height, 8, LANES), F32),
            pltpu.SMEM(offsets.shape, jnp.int32),
            pltpu.SMEM(scale.shape, F32),
            pltpu.SemaphoreType.DMA((2,)),
        ],
        compiler_params=pltpu.CompilerParams(vmem_limit_bytes=24 << 20),
        cost_estimate=pl.CostEstimate(flops=10**9, bytes_accessed=10**7, transcendentals=10**5),
        name="sums",
    )(offsets, scale, group, scores, particles)


def mean_body(shifts, offs, lhs_ref, bank_ref, keep_ref, other_ref, out_ref, sum_ref):
    rows = out_ref.shape[1] // LANES
    step_rows = 2 if rows % 2 == 0 else 1
    people = out_ref.shape[0]
    lefts = lhs_ref[0]

    @pl.when(pl.program_id(0) == 0)
    def _():
        out_ref[...] = jnp.zeros_like(out_ref)
        sum_ref[...] = keep_ref[...] + other_ref[...]

    def step(j, carry):
        y = j * step_rows
        his, los = [], []
        for t in range(shifts):
            b = offs[1, t] + REACH
            r = y + REACH - offs[0, t]
            tiles = [bank_ref[0, b, r + e] for e in range(step_rows)]
            tile = jnp.concatenate(tiles, axis=1) if step_rows > 1 else tiles[0]
            his.append(tile[:32])
            los.append(tile[32:])
        both = jnp.dot(lefts, jnp.concatenate(his, axis=0), preferred_element_type=F32)
        rest = jnp.dot(lefts[:people], jnp.concatenate(los, axis=0), preferred_element_type=F32)
        at = pl.ds(pl.multiple_of(y * LANES, step_rows * LANES), step_rows * LANES)
        out_ref[:, at] += both[:people] + both[people:] + rest
        return carry

    lax.fori_loop(0, rows // step_rows, step, 0, unroll=min(8, rows // step_rows))


def mean_call(lefts, bank, offsets, people, keep, other):
    shifts = offsets.shape[1]
    groups, span, tall, wide, lanes = bank.shape
    width = (tall - 2 * REACH) * LANES
    smem = pl.BlockSpec(memory_space=pltpu.SMEM)
    return pl.pallas_call(
        functools.partial(mean_body, shifts),
        grid=(groups,),
        out_shape=(
            jax.ShapeDtypeStruct((people, width), F32),
            jax.ShapeDtypeStruct(keep.shape, F32),
        ),
        in_specs=[
            smem,
            pl.BlockSpec((1,) + lefts.shape[1:], lambda g: (g, 0, 0)),
            pl.BlockSpec((1, span, tall, wide, lanes), lambda g: (g, 0, 0, 0, 0)),
            pl.BlockSpec(keep.shape, lambda g: (0, 0)),
            pl.BlockSpec(keep.shape, lambda g: (0, 0)),
        ],
        out_specs=(
            pl.BlockSpec((people, width), lambda g: (0, 0)),
            pl.BlockSpec(keep.shape, lambda g: (0, 0)),
        ),
        compiler_params=pltpu.CompilerParams(vmem_limit_bytes=20 << 20),
        cost_estimate=pl.CostEstimate(flops=10**9, bytes_accessed=10**7, transcendentals=0),
        name="mean",
    )(offsets, lefts, bank, keep, other)


def local(particles, references, shift_offsets, particle_group, group_scale):
    people, pixels = particles.shape
    count = lax.axis_size("refs")
    rows = pixels // LANES
    own = rows // count
    assert references.shape[0] == 4 and people * 4 == LANES and count % 8 == 0
    assert shift_offsets.shape[0] <= 32 and lax.axis_size("parts") == 2
    me = lax.axis_index("refs")
    offsets = shift_offsets.T
    bits = []
    d = count // 2
    while d:
        bits.append(d)
        d //= 2

    def swap(value, d):
        return lax.ppermute(value, "refs", [(i, i ^ d) for i in range(count)])

    slab_order = [0]
    for step, d in enumerate(bits):
        if step == 0:
            keep, send = front_call(references, d, own)
        else:
            side = (me // d) % 2
            wide = (d * own + 2 * REACH) * LANES
            jump = d * own * LANES
            keep = lax.dynamic_slice_in_dim(slab, side * jump, wide, 1)
            send = lax.dynamic_slice_in_dim(slab, (1 - side) * jump, wide, 1)
        slab = jnp.concatenate([keep, swap(send, d)], axis=0)
        slab_order += [m ^ d for m in slab_order]
    bank = bank_call(slab)

    scores = score_call(particles, references, offsets)[None]
    order = [0]
    for d in bits[-1:] + bits[:-1]:
        scores = jnp.concatenate([scores, swap(scores, d)], axis=0)
        order += [m ^ d for m in order]
    places = [order.index(m) for m in slab_order]

    group = particle_group.reshape(1, people)
    lefts, keep, send = sums_call(places, scores, particles, offsets, group, group_scale)
    other = lax.ppermute(send, "parts", [(0, 1), (1, 0)])
    return mean_call(lefts, bank, offsets, people, keep, other)


def solution(mesh):
    return jax.shard_map(
        local,
        mesh=mesh,
        in_specs=(
            P(("groups", "parts"), None),
            P(("groups", "refs"), None),
            P("groups", None),
            P(("groups", "parts")),
            P(),
        ),
        out_specs=(P(("groups", "parts"), "refs"), P(("groups", "refs"), "parts")),
        check_vma=False,
    )
```
